32 devices in a mesh: dp: 8 (over z, y), mp: 4 (over x, core).
Axes of the slice: x: 2, y: 2, z: 4, core: 2. Of those that a mesh axis runs over, the one named last changes fastest.
Arguments:
- tokens: bfloat16 [2048, 1152], P('dp'), may hold values from -6 to 6
- conditioning: bfloat16 [4, 1152], replicated, may hold values from -6 to 6
- segments: int32 [2048], P('dp'), may hold values from 0 to 3, never falling along the last dimension, each value on 1 to 1024 neighbouring positions
- live_counts: int32 [8], P('dp'), may hold values from 32 to 256, as said below
- attn_weight: bfloat16 [3, 1152, 1152], P(None, 'dp', 'mp')
- attn_bias: float32 [2, 1152], P(None, 'mp'), may hold values from -3 to 3
- out_weight: bfloat16 [1152, 1152], P('mp', 'dp'), may hold values from -4 to 4
- out_bias: float32 [1152], replicated, may hold values from -3 to 3
- up_weight: bfloat16 [1152, 4608], P('dp', 'mp'), may hold values from -0.1875 to 0.1875
- up_bias: float32 [4608], P('mp'), may hold values from -3 to 3
- down_weight: bfloat16 [4608, 1152], P('mp', 'dp'), may hold values from -0.1875 to 0.1875
- down_bias: float32 [1152], replicated, may hold values from -3 to 3
- mod_weight: bfloat16 [1152, 6912], P('dp', 'mp'), may hold values from -0.1875 to 0.1875
- mod_bias: float32 [6912], P('mp'), may hold values from -3 to 3
- cotangent: bfloat16 [2048, 1152], P('dp'), may hold values from -6 to 6
Outputs:
- result: bfloat16 [2048, 1152], P(('dp', 'mp'))
- grad_tokens: float32 [2048, 1152], P(('dp', 'mp'))
- grad_conditioning: float32 [4, 1152], replicated
- grad_attn_weight: float32 [3, 1152, 1152], P(None, 'dp', 'mp')
- grad_attn_bias: float32 [2, 1152], P(None, 'mp')
- grad_out_weight: float32 [1152, 1152], P('mp', 'dp')
- grad_out_bias: float32 [1152], replicated
- grad_up_weight: float32 [1152, 4608], P('dp', 'mp')
- grad_up_bias: float32 [4608], P('mp')
- grad_down_weight: float32 [4608, 1152], P('mp', 'dp')
- grad_down_bias: float32 [1152], replicated
- grad_mod_weight: float32 [1152, 6912], P('dp', 'mp')
- grad_mod_bias: float32 [6912], P('mp')
The draws below stay inside these ranges and needn't reach their ends.
Inputs may be any that keep to these rules, and one draw needn't show every extreme that they name: `segments`: the tokens of each latent stand next to each other; no latent has more than 1024 tokens and some latent has exactly 1024. The first live_counts[i] rows of index i of dp are live; some index has 256 and some other has 32.
All inputs are finite; a program needn't handle non-finite values.
Results may differ from the reference program's by a relative error of at most 0.017.
The reference program's roundings to bfloat16 on the way count: a program that leaves them out, or rounds other values in their place, can miss the bound.
Values may be sent and summed in bfloat16 or wider, within the bound.
No kernel may reach another device: no remote copies, remote signals or barrier semaphores. Data moves between devices by JAX's collectives and lax.ppermute only.
A program may use at most 192 MiB of HBM per device.

```python
import math
import jax
import jax.numpy as jnp
import numpy as np
from jax import lax

D = 1152
H = 16
FF = 4608
HD = 72
TOK_DEV = 256
SEG_MOST = 1024
REACH = 4
TOKENS = 2048
LATENTS = 4
N_DP = 8


def draw_live_counts(key, part):
    values = jax.random.randint(key, (N_DP,), TOK_DEV // 8, TOK_DEV + 1)
    first = jax.random.randint(jax.random.fold_in(key, 11), (), 0, N_DP)
    second = (first + 1 + jax.random.randint(jax.random.fold_in(key, 12), (), 0, N_DP - 1)) % N_DP
    values = values.at[first].set(TOK_DEV).at[second].set(TOK_DEV // 8)
    return values.astype(jnp.int32)


def draw_attn_weight(key, part):
    base = jnp.clip(jax.random.normal(key, (3, D, D), jnp.float32), -5.0, 5.0) / math.sqrt(D)
    return base.astype(jnp.bfloat16)


def block_levels(stream_key, shape, pieces, least, high):
    def one(axis_at, shards_of):
        steps = jax.random.uniform(jax.random.fold_in(jax.random.fold_in(stream_key, 6), axis_at), (shards_of,), jnp.float32, least / len(pieces), high / len(pieces))
        return jnp.repeat(jnp.exp(steps), shape[axis_at] // shards_of).reshape((-1,) + (1,) * (len(shape) - axis_at - 1))

    gain = one(*pieces[0])
    for cut in pieces[1:]:
        gain = gain * one(*cut)
    return gain


def split_up(count, total, most, lean):
    loads = [(1 << 20) // math.isqrt(rank ** lean) + 1 for rank in range(2, count + 1)]
    rest, holding = total - most - (count - 1), [1] * (count - 1)
    while rest > 0:
        movable = [i for i in range(count - 1) if holding[i] < most]
        mass, left = sum([loads[i] for i in movable]), rest
        for i in movable:
            more = min(most - holding[i], max(1, left * loads[i] // mass), rest)
            holding[i] = holding[i] + more
            rest = rest - more
    return np.array([most] + holding)


def uneven_parts(key, number_of, total, limit, lean):
    if number_of == 2:
        one = jax.random.randint(key, (), max(1, total - limit), min(limit, total - 1) + 1)
        return jnp.stack([one, total - one])
    lengths = jnp.asarray(split_up(number_of, total, limit, lean), jnp.int32)
    couples = (number_of - 1) // 2
    giver, receiver = lengths[1:1 + 2 * couples:2], lengths[2:2 + 2 * couples:2]
    room = jnp.minimum(giver - 1, limit - receiver)
    shifted = jax.random.randint(jax.random.fold_in(key, 1), (couples,), 0, 1 << 20) % (room + 1)
    lengths = lengths.at[1:1 + 2 * couples:2].set(giver - shifted).at[2:2 + 2 * couples:2].set(receiver + shifted)
    return lengths[jax.random.permutation(jax.random.fold_in(key, 2), number_of)]


def scatter_about(own_key, dims, scale, most, cuts=(), kind=jnp.bfloat16):
    drawn = jax.random.normal(own_key, dims, jnp.float32) * scale
    if len(cuts) > 0:
        drawn = block_levels(own_key, dims, cuts, -0.22, 0.18) * drawn
    return jnp.clip(drawn, min=-most, max=most).astype(kind)


def setup_inputs(seed: int = 0) -> dict:
    keys = jax.random.split(jax.random.key(seed), 16)
    tokens = scatter_about(keys[0], (TOKENS, D), 1.0, 6.0, ((0, 8),))
    conditioning = scatter_about(keys[1], (LATENTS, D), 1.0, 6.0)
    segments = jnp.searchsorted(jnp.cumsum(uneven_parts(keys[2], LATENTS, TOKENS, SEG_MOST, 2)), jnp.arange(TOKENS), side="right").astype(jnp.int32)
    live_counts = draw_live_counts(jax.random.fold_in(keys[15], 71), 0)
    attn_weight = draw_attn_weight(jax.random.fold_in(keys[15], 71), 0)
    attn_bias = scatter_about(keys[5], (2, D), 0.5, 3.0, ((1, 4),), jnp.float32)
    out_weight = scatter_about(keys[6], (D, D), (max(D // 512, 1)) ** -0.5, 4.0, ((0, 4), (1, 8)))
    out_bias = scatter_about(keys[7], (D,), 0.5, 3.0, (), jnp.float32)
    up_weight = scatter_about(keys[8], (D, FF), D ** -0.5, 0.1875, ((0, 8), (1, 4)))
    up_bias = scatter_about(keys[9], (FF,), 0.5, 3.0, ((0, 4),), jnp.float32)
    down_weight = scatter_about(keys[10], (FF, D), (FF // 4) ** -0.5, 0.1875, ((0, 4), (1, 8)))
    down_bias = scatter_about(keys[11], (D,), 0.5, 3.0, (), jnp.float32)
    mod_weight = scatter_about(keys[12], (D, 6 * D), D ** -0.5, 0.1875, ((0, 8), (1, 4)))
    mod_bias = scatter_about(keys[13], (6 * D,), 0.5, 3.0, ((0, 4),), jnp.float32)
    cotangent = scatter_about(keys[14], (TOKENS, D), 1.0, 6.0, ((0, 8),))
    return dict(tokens=tokens, conditioning=conditioning, segments=segments, live_counts=live_counts, attn_weight=attn_weight, attn_bias=attn_bias, out_weight=out_weight, out_bias=out_bias, up_weight=up_weight, up_bias=up_bias, down_weight=down_weight, down_bias=down_bias, mod_weight=mod_weight, mod_bias=mod_bias, cotangent=cotangent)


EPSILON = 1e-06
NEG_FILL = -1e+30

def normalize(values):
    average = lax.optimization_barrier(jnp.mean(values, axis=-1, keepdims=True))
    centered = values - average
    spread_sq = lax.optimization_barrier(jnp.mean(centered * centered, axis=-1, keepdims=True))
    inv_std = lax.rsqrt(spread_sq + EPSILON)
    return (centered * inv_std, inv_std)

def normalize_back(grad_hat, normed, inv_std):
    first = lax.optimization_barrier(jnp.mean(grad_hat, axis=-1, keepdims=True))
    second = lax.optimization_barrier(jnp.mean(grad_hat * normed, axis=-1, keepdims=True))
    return inv_std * (grad_hat - first - normed * second)

def gelu_tanh(values):
    return jax.nn.gelu(values, approximate=True)

def silu_slope(values):
    sigma = jax.nn.sigmoid(values)
    return sigma * (1.0 + values * (1.0 - sigma))

def reference(tokens, conditioning, segments, live_counts, attn_weight, attn_bias, out_weight, out_bias, up_weight, up_bias, down_weight, down_bias, mod_weight, mod_bias, cotangent):
    score_scale = 1.0 / HD ** 0.5
    position = jnp.arange(TOKENS, dtype=jnp.int32)
    live = (position % TOK_DEV < live_counts[position // TOK_DEV]).astype(jnp.float32)[:, None]
    token_vals = tokens.astype(jnp.float32)
    cond_vals = conditioning.astype(jnp.float32)
    silu_cond = jax.nn.silu(cond_vals).astype(jnp.bfloat16)
    modulation = jnp.dot(silu_cond, mod_weight, preferred_element_type=jnp.float32) + mod_bias
    per_token = modulation[segments]
    shift_attn, scale_attn, gate_attn, shift_mlp, scale_mlp, gate_mlp = jnp.split(per_token, 6, axis=1)
    normed_one, inv_one = normalize(token_vals)
    attn_input = (normed_one * (1.0 + scale_attn) + shift_attn).astype(jnp.bfloat16)
    query_rows = (jnp.dot(attn_input, attn_weight[0], preferred_element_type=jnp.float32) + attn_bias[0]).astype(jnp.bfloat16)
    key_rows = jnp.dot(attn_input, attn_weight[1], preferred_element_type=jnp.float32).astype(jnp.bfloat16)
    value_rows = (jnp.dot(attn_input, attn_weight[2], preferred_element_type=jnp.float32) + attn_bias[1]).astype(jnp.bfloat16)
    margin = REACH * TOK_DEV
    window = (2 * REACH + 1) * TOK_DEV
    query_tag = segments + 1
    key_tag = jnp.where(live[:, 0] > 0.0, segments + 1, 0).astype(jnp.int32)
    key_pad = jnp.pad(key_rows, ((margin, margin), (0, 0))).reshape(-1, H, HD)
    value_pad = jnp.pad(value_rows, ((margin, margin), (0, 0))).reshape(-1, H, HD)
    tag_pad = jnp.pad(key_tag, (margin, margin))
    query_heads = query_rows.reshape(TOKENS, H, HD)
    self_mask = jnp.arange(window, dtype=jnp.int32)[None, :] == (margin + jnp.arange(TOK_DEV, dtype=jnp.int32))[:, None]

    def block_scores(index):
        start = (index * TOK_DEV).astype(jnp.int32)
        query_blk = lax.dynamic_slice_in_dim(query_heads, start, TOK_DEV, 0)
        key_blk = lax.dynamic_slice_in_dim(key_pad, start, window, 0)
        value_blk = lax.dynamic_slice_in_dim(value_pad, start, window, 0)
        tag_blk = lax.dynamic_slice_in_dim(tag_pad, start, window, 0)
        qtag_blk = lax.dynamic_slice_in_dim(query_tag, start, TOK_DEV, 0)
        allowed = (tag_blk[None, :] == qtag_blk[:, None]) | self_mask
        scores = jnp.einsum('qhd,khd->hqk', query_blk.astype(jnp.float32), key_blk.astype(jnp.float32)) * score_scale
        scores = jnp.where(allowed[None], scores, NEG_FILL)
        return (query_blk, key_blk, value_blk, scores)

    def forward_block(index):
        query_blk, key_blk, value_blk, scores = block_scores(index)
        row_max = lax.optimization_barrier(jnp.max(scores, axis=-1, keepdims=True))
        log_total = row_max + jnp.log(lax.optimization_barrier(jnp.sum(jnp.exp(scores - row_max), axis=-1, keepdims=True)))
        attn_probs = jnp.exp(scores - log_total).astype(jnp.bfloat16)
        attended_blk = jnp.einsum('hqk,khd->qhd', attn_probs.astype(jnp.float32), value_blk.astype(jnp.float32))
        return (attended_blk.astype(jnp.bfloat16).reshape(TOK_DEV, D), log_total)
    attended, log_totals = lax.map(forward_block, jnp.arange(N_DP, dtype=jnp.int32))
    attended = attended.reshape(TOKENS, D)
    attn_out = jnp.dot(attended, out_weight, preferred_element_type=jnp.float32) + out_bias
    mid = token_vals + live * gate_attn * attn_out
    normed_two, inv_two = normalize(mid)
    mlp_input = (normed_two * (1.0 + scale_mlp) + shift_mlp).astype(jnp.bfloat16)
    hidden_pre = jnp.dot(mlp_input, up_weight, preferred_element_type=jnp.float32) + up_bias
    hidden = gelu_tanh(hidden_pre).astype(jnp.bfloat16)
    mlp_out = jnp.dot(hidden, down_weight, preferred_element_type=jnp.float32) + down_bias
    result = (mid + live * gate_mlp * mlp_out).astype(jnp.bfloat16)
    grad_result = cotangent.astype(jnp.float32)
    grad_mlp = grad_result * live * gate_mlp
    grad_mlp_b = grad_mlp.astype(jnp.bfloat16)
    grad_down_weight = jnp.dot(hidden.T, grad_mlp_b, preferred_element_type=jnp.float32)
    grad_down_bias = lax.optimization_barrier(jnp.sum(grad_mlp, axis=0))
    grad_hidden = jnp.dot(grad_mlp_b, down_weight.T, preferred_element_type=jnp.float32)
    grad_pre = jax.vjp(gelu_tanh, hidden_pre)[1](grad_hidden)[0]
    grad_pre_b = grad_pre.astype(jnp.bfloat16)
    grad_up_bias = lax.optimization_barrier(jnp.sum(grad_pre, axis=0))
    grad_up_weight = jnp.dot(mlp_input.T, grad_pre_b, preferred_element_type=jnp.float32)
    grad_mlp_in = jnp.dot(grad_pre_b, up_weight.T, preferred_element_type=jnp.float32)
    grad_mid = grad_result + normalize_back(grad_mlp_in * (1.0 + scale_mlp), normed_two, inv_two)
    grad_attn = grad_mid * live * gate_attn
    grad_attn_b = grad_attn.astype(jnp.bfloat16)
    grad_out_weight = jnp.dot(attended.T, grad_attn_b, preferred_element_type=jnp.float32)
    grad_out_bias = lax.optimization_barrier(jnp.sum(grad_attn, axis=0))
    grad_attended = jnp.dot(grad_attn_b, out_weight.T, preferred_element_type=jnp.float32).astype(jnp.bfloat16)
    grad_att_heads = grad_attended.reshape(TOKENS, H, HD)
    attended_heads = attended.reshape(TOKENS, H, HD)

    def backward_block(carry, index):
        key_grad_pad, value_grad_pad = carry
        query_blk, key_blk, value_blk, scores = block_scores(index)
        start = (index * TOK_DEV).astype(jnp.int32)
        log_total = log_totals[index]
        grad_blk = lax.dynamic_slice_in_dim(grad_att_heads, start, TOK_DEV, 0).astype(jnp.float32)
        att_blk = lax.dynamic_slice_in_dim(attended_heads, start, TOK_DEV, 0).astype(jnp.float32)
        attn_exact = jnp.exp(scores - log_total)
        attn_probs = attn_exact.astype(jnp.bfloat16)
        grad_probs = jnp.einsum('qhd,khd->hqk', grad_blk, value_blk.astype(jnp.float32))
        delta = lax.optimization_barrier(jnp.sum(grad_blk * att_blk, axis=-1))
        grad_scores = (attn_exact * (grad_probs - jnp.transpose(delta)[:, :, None])).astype(jnp.bfloat16)
        grad_query_blk = jnp.einsum('hqk,khd->qhd', grad_scores.astype(jnp.float32), key_blk.astype(jnp.float32)) * score_scale
        grad_key_blk = jnp.einsum('hqk,qhd->khd', grad_scores.astype(jnp.float32), query_blk.astype(jnp.float32)) * score_scale
        grad_value_blk = jnp.einsum('hqk,qhd->khd', attn_probs.astype(jnp.float32), grad_blk)
        key_grad_pad = lax.dynamic_update_slice_in_dim(key_grad_pad, lax.dynamic_slice_in_dim(key_grad_pad, start, window, 0) + grad_key_blk, start, 0)
        value_grad_pad = lax.dynamic_update_slice_in_dim(value_grad_pad, lax.dynamic_slice_in_dim(value_grad_pad, start, window, 0) + grad_value_blk, start, 0)
        return ((key_grad_pad, value_grad_pad), grad_query_blk.reshape(TOK_DEV, D))
    zero_pad = jnp.zeros((TOKENS + 2 * margin, H, HD), jnp.float32)
    (key_grad_pad, value_grad_pad), grad_query = lax.scan(backward_block, (zero_pad, zero_pad), jnp.arange(N_DP, dtype=jnp.int32))
    grad_query = grad_query.reshape(TOKENS, D)
    grad_keyed = key_grad_pad[margin:margin + TOKENS].reshape(TOKENS, D)
    grad_value = value_grad_pad[margin:margin + TOKENS].reshape(TOKENS, D)
    grad_attn_bias = jnp.stack([lax.optimization_barrier(jnp.sum(grad_query, axis=0)), lax.optimization_barrier(jnp.sum(grad_value, axis=0))])
    grad_qkv = jnp.stack([grad_query, grad_keyed, grad_value]).astype(jnp.bfloat16)
    grad_attn_weight = jnp.stack([jnp.dot(attn_input.T, grad_qkv[which], preferred_element_type=jnp.float32) for which in range(3)])
    grad_attn_in = jnp.dot(grad_qkv[0], attn_weight[0].T, preferred_element_type=jnp.float32)
    grad_attn_in = grad_attn_in + jnp.dot(grad_qkv[1], attn_weight[1].T, preferred_element_type=jnp.float32)
    grad_attn_in = grad_attn_in + jnp.dot(grad_qkv[2], attn_weight[2].T, preferred_element_type=jnp.float32)
    grad_tokens = grad_mid + normalize_back(grad_attn_in * (1.0 + scale_attn), normed_one, inv_one)
    grad_mod_rows = jnp.concatenate([grad_attn_in, grad_attn_in * normed_one, grad_mid * live * attn_out, grad_mlp_in, grad_mlp_in * normed_two, grad_result * live * mlp_out], axis=1)
    grad_modulation = jax.ops.segment_sum(grad_mod_rows, segments, num_segments=LATENTS)
    grad_mod_weight = jnp.dot(silu_cond.astype(jnp.float32).T, grad_modulation, precision=lax.Precision.HIGHEST)
    grad_mod_bias = lax.optimization_barrier(jnp.sum(grad_modulation, axis=0))
    grad_silu = jnp.dot(grad_modulation, mod_weight.astype(jnp.float32).T, precision=lax.Precision.HIGHEST)
    grad_conditioning = grad_silu * silu_slope(cond_vals)
    return (result, grad_tokens, grad_conditioning, grad_attn_weight, grad_attn_bias, grad_out_weight, grad_out_bias, grad_up_weight, grad_up_bias, grad_down_weight, grad_down_bias, grad_mod_weight, grad_mod_bias)
```

```python
import jax
import jax.numpy as jnp
from jax import lax
from jax.sharding import Mesh
from jax.sharding import PartitionSpec as P

HD = 72
KV_ROWS = 152
BLOCK = 4

EPSILON = 1e-06
NEG_FILL = -1e30
DP = ("da", "db")
ALL = ("da", "db", "mp")
BF = jnp.bfloat16
F32 = jnp.float32


def normalize(values):
    average = jnp.mean(values, axis=-1, keepdims=True)
    centered = values - average
    spread_sq = jnp.mean(centered * centered, axis=-1, keepdims=True)
    inv_std = lax.rsqrt(spread_sq + EPSILON)
    return (centered * inv_std, inv_std)


def normalize_back(grad_hat, normed, inv_std):
    first = jnp.mean(grad_hat, axis=-1, keepdims=True)
    second = jnp.mean(grad_hat * normed, axis=-1, keepdims=True)
    return inv_std * (grad_hat - first - normed * second)


def gelu_tanh(values):
    return jax.nn.gelu(values, approximate=True)


def silu_slope(values):
    sigma = jax.nn.sigmoid(values)
    return sigma * (1.0 + values * (1.0 - sigma))


def dot(left, right, left_dim, right_dim, **kw):
    return lax.dot_general(
        left, right, (((left_dim,), (right_dim,)), ((), ())), preferred_element_type=F32, **kw
    )


def scatter_rows(partial):
    rows, width = partial.shape
    member = lax.axis_index("mp")
    low, high = member % 2, member // 2
    halves = partial.reshape(2, 2, rows // 4, width)
    keep = lax.dynamic_index_in_dim(halves, low, 1, keepdims=False)
    give = lax.dynamic_index_in_dim(halves, 1 - low, 1, keepdims=False).astype(BF)
    kept = keep + lax.ppermute(give, "mp", [(m, m ^ 1) for m in range(4)]).astype(F32)
    keep = lax.dynamic_index_in_dim(kept, high, 0, keepdims=False)
    give = lax.dynamic_index_in_dim(kept, 1 - high, 0, keepdims=False).astype(BF)
    return keep + lax.ppermute(give, "mp", [(m, m ^ 2) for m in range(4)]).astype(F32)


def neighbours(block_kv, blocks):
    if blocks == 2:
        return [lax.ppermute(block_kv, "da", [(0, 1), (1, 0)])]
    return [
        lax.ppermute(block_kv, "da", [(i, i + 1) for i in range(blocks - 1)]),
        lax.ppermute(block_kv, "da", [(i + 1, i) for i in range(blocks - 1)]),
    ]


def return_grads(pieces, blocks):
    if blocks == 2:
        return lax.ppermute(pieces[0], "da", [(0, 1), (1, 0)]).astype(F32)
    return lax.ppermute(pieces[0], "da", [(i + 1, i) for i in range(blocks - 1)]).astype(
        F32
    ) + lax.ppermute(pieces[1], "da", [(i, i + 1) for i in range(blocks - 1)]).astype(F32)


def shards(
    tokens,
    conditioning,
    segments,
    live_counts,
    attn_weight,
    attn_bias,
    out_weight,
    out_bias,
    up_weight,
    up_bias,
    down_weight,
    down_bias,
    mod_weight,
    mod_bias,
    cotangent,
):
    tok_rows, width = tokens.shape
    latents = conditioning.shape[0]
    columns = attn_weight.shape[2]
    heads_here = columns // HD
    weight_rows = up_weight.shape[0]
    hidden_cols = up_bias.shape[0]
    mod_cols = mod_bias.shape[0]
    score_scale = 1.0 / HD**0.5
    blocks = lax.axis_size("da")
    group = lax.axis_size("mp")
    n_dp = blocks * BLOCK
    share = tok_rows // group
    member = lax.axis_index("mp")
    block_at = lax.axis_index("db")
    dp_at = lax.axis_index("da") * BLOCK + block_at
    row_start = member * share
    block_rows = BLOCK * tok_rows

    def own_rows(values):
        return lax.dynamic_slice_in_dim(values, row_start, share, 0)

    attn_local = jnp.transpose(
        attn_weight.reshape(3, weight_rows, heads_here, HD), (1, 2, 0, 3)
    )
    attn_local = attn_local[:, :, jnp.array([1, 2, 0])].reshape(weight_rows, 3 * columns)
    attn_full = lax.all_gather(attn_local, DP, axis=0, tiled=True)
    out_t = lax.all_gather(out_weight.T, DP, axis=0, tiled=True)
    up_full = lax.all_gather(up_weight, DP, axis=0, tiled=True)
    down_t = lax.all_gather(down_weight.T, DP, axis=0, tiled=True)

    cond_vals = conditioning.astype(F32)
    silu_cond = jax.nn.silu(cond_vals).astype(BF)
    silu_own = lax.dynamic_slice_in_dim(silu_cond, dp_at * weight_rows, weight_rows, 1)
    mod_part = dot(silu_own, mod_weight, 1, 0)
    mod_part = mod_part + jnp.where(dp_at == 0, 1.0, 0.0) * mod_bias
    mod_parts = lax.all_gather(mod_part, ALL, axis=0, tiled=False)
    modulation = jnp.sum(mod_parts.reshape(n_dp, group, latents, mod_cols), axis=0)
    modulation = jnp.transpose(modulation, (1, 0, 2)).reshape(latents, 6 * width)
    one_hot = (segments[:, None] == jnp.arange(latents, dtype=jnp.int32)[None, :]).astype(F32)
    one_hot_s = own_rows(one_hot)

    def modulate(hot, first, last):
        return jnp.dot(
            hot, modulation[:, first * width : last * width], precision=lax.Precision.HIGHEST
        )

    shift_attn, scale_attn = jnp.split(modulate(one_hot, 0, 2), 2, axis=1)
    gate_mlp = modulate(one_hot, 5, 6)
    scale_attn_s, gate_attn_s, shift_mlp_s, scale_mlp_s, gate_mlp_s = jnp.split(
        modulate(one_hot_s, 1, 6), 5, axis=1
    )
    live = (jnp.arange(tok_rows, dtype=jnp.int32) < live_counts[0]).astype(F32)[:, None]
    live_s = own_rows(live)
    token_vals = tokens.astype(F32)
    token_s = own_rows(token_vals)
    normed_one, inv_one = normalize(token_vals)
    attn_input = (normed_one * (1.0 + scale_attn) + shift_attn).astype(BF)

    head_bias = attn_bias.reshape(2, heads_here, HD)
    bias_t = jnp.stack([jnp.zeros_like(head_bias[0]), head_bias[1], head_bias[0]], axis=1)
    kvq_t = (dot(attn_full, attn_input, 0, 1) + bias_t.reshape(3 * columns)[:, None]).astype(BF)
    kvq_t = kvq_t.reshape(heads_here, 3 * HD, tok_rows)
    tags = jnp.stack(
        [jnp.where(live[:, 0] > 0.0, segments + 1, 0).astype(BF), (segments + 1).astype(BF)]
    )
    tags = jnp.pad(tags, ((0, KV_ROWS - 2 * HD - 2), (0, 0)))
    tags = jnp.broadcast_to(tags[None], (heads_here,) + tags.shape)
    sent = jnp.concatenate([kvq_t[:, : 2 * HD], tags, kvq_t[:, 2 * HD :]], axis=1)
    got = lax.all_to_all(sent, "db", 0, 0)
    kv_own = got[:, :KV_ROWS]
    kv_all = jnp.stack([kv_own] + neighbours(kv_own, blocks))
    key_blocks = kv_all.shape[0]
    keys_seen = key_blocks * block_rows
    kv_t = jnp.transpose(kv_all, (2, 0, 1, 3)).reshape(KV_ROWS, keys_seen)
    key_t, value_t = kv_t[:HD], kv_t[HD : 2 * HD]
    key_tag = kv_t[2 * HD].astype(F32)
    query_tag = kv_t[2 * HD + 1, :block_rows].astype(F32)
    query_t = jnp.transpose(got[:, KV_ROWS:], (1, 0, 2)).reshape(HD, block_rows)
    self_mask = (
        jnp.arange(keys_seen, dtype=jnp.int32)[None, :]
        == jnp.arange(block_rows, dtype=jnp.int32)[:, None]
    )
    allowed = (key_tag[None, :] == query_tag[:, None]) | self_mask

    def masked_scores():
        return jnp.where(allowed, dot(query_t, key_t, 0, 0) * score_scale, NEG_FILL)

    scores = masked_scores()
    row_max = jnp.max(scores, axis=-1, keepdims=True)
    log_total = row_max + jnp.log(jnp.sum(jnp.exp(scores - row_max), axis=-1, keepdims=True))
    attn_exact = jnp.exp(scores - log_total)
    attn_probs = attn_exact.astype(BF)
    head_attended = dot(value_t, attn_probs, 1, 1).astype(BF)

    def to_owners(head_rows):
        rows = head_rows.shape[0]
        parts = jnp.transpose(head_rows.reshape(rows, BLOCK, tok_rows), (1, 0, 2))
        return lax.all_to_all(parts, "db", 0, 0).reshape(heads_here * rows, tok_rows)

    attended_t = to_owners(head_attended)
    attn_out_s = scatter_rows(dot(attended_t, out_t, 0, 1)) + out_bias
    mid_s = token_s + live_s * gate_attn_s * attn_out_s
    normed_two_s, inv_two_s = normalize(mid_s)
    mlp_input_s = (normed_two_s * (1.0 + scale_mlp_s) + shift_mlp_s).astype(BF)
    mlp_input = lax.all_gather(mlp_input_s, "mp", axis=0, tiled=True)
    hidden_pre = dot(mlp_input, up_full, 1, 0) + up_bias
    hidden = gelu_tanh(hidden_pre).astype(BF)

    grad_result = cotangent.astype(F32)
    grad_result_s = own_rows(grad_result)
    grad_mlp = grad_result * live * gate_mlp
    grad_mlp_b = grad_mlp.astype(BF)
    grad_hidden = dot(grad_mlp_b, down_t, 1, 0)
    grad_pre = jax.vjp(gelu_tanh, hidden_pre)[1](grad_hidden)[0]
    grad_pre_b = grad_pre.astype(BF)
    grad_mlp_in_s = scatter_rows(dot(grad_pre_b, up_full, 1, 1))
    grad_mid_s = grad_result_s + normalize_back(
        grad_mlp_in_s * (1.0 + scale_mlp_s), normed_two_s, inv_two_s
    )
    grad_attn_s = grad_mid_s * live_s * gate_attn_s
    grad_attn_b = lax.all_gather(grad_attn_s.astype(BF), "mp", axis=0, tiled=True)
    grad_down_w = dot(grad_mlp_b, hidden, 0, 0)
    grad_up_w = dot(mlp_input, grad_pre_b, 0, 0)
    mlp_w = lax.psum_scatter(
        jnp.concatenate([grad_up_w.astype(BF), grad_down_w.astype(BF)], axis=1),
        DP,
        scatter_dimension=0,
        tiled=True,
    ).astype(F32)
    up_w_out, down_w_out = mlp_w[:, :hidden_cols], mlp_w[:, hidden_cols:].T
    mlp_out_s = scatter_rows(dot(hidden, down_t, 1, 1)) + down_bias
    result_s = (mid_s + live_s * gate_mlp_s * mlp_out_s).astype(BF)

    grad_attended_t = dot(out_t, grad_attn_b, 0, 1).astype(BF)
    got_grad = lax.all_to_all(grad_attended_t.reshape(heads_here, HD, tok_rows), "db", 0, 0)
    grad_t = jnp.transpose(got_grad, (1, 0, 2)).reshape(HD, block_rows)
    grad_probs = dot(grad_t, value_t, 0, 0)
    delta = jnp.sum(grad_t.astype(F32) * head_attended.astype(F32), axis=0)[:, None]
    grad_scores = (attn_exact * (grad_probs - delta)).astype(BF)
    grad_query_t = dot(key_t, grad_scores, 1, 1) * score_scale
    grad_key_t = dot(query_t, grad_scores, 1, 0) * score_scale
    grad_value_t = dot(grad_t, attn_probs, 1, 0)
    grad_kv_t = jnp.concatenate([grad_key_t, grad_value_t])
    others = [
        grad_kv_t[:, i * block_rows : (i + 1) * block_rows].astype(BF)
        for i in range(1, key_blocks)
    ]
    grad_kv_own = grad_kv_t[:, :block_rows] + return_grads(others, blocks)
    attn_b_part = jnp.concatenate(
        [jnp.sum(grad_query_t, axis=1), jnp.sum(grad_kv_own[HD:], axis=1)]
    )
    grad_kvq_t = to_owners(jnp.concatenate([grad_kv_own, grad_query_t]).astype(BF))
    grad_attn_w = dot(attn_input, grad_kvq_t, 0, 1)
    grad_out_w = dot(grad_attn_b, attended_t, 0, 1)
    attn_w = lax.psum_scatter(
        jnp.concatenate([grad_attn_w.astype(BF), grad_out_w.astype(BF)], axis=1),
        DP,
        scatter_dimension=0,
        tiled=True,
    ).astype(F32)
    out_w_out = attn_w[:, 3 * columns :].T
    attn_w_out = attn_w[:, : 3 * columns].reshape(weight_rows, heads_here, 3, HD)
    attn_w_out = jnp.transpose(attn_w_out[:, :, jnp.array([2, 0, 1])], (2, 0, 1, 3)).reshape(
        3, weight_rows, columns
    )
    grad_attn_in_s = scatter_rows(dot(grad_kvq_t, attn_full, 0, 1))
    normed_one_s = own_rows(normed_one)
    inv_one_s = own_rows(inv_one)
    grad_tokens_s = grad_mid_s + normalize_back(
        grad_attn_in_s * (1.0 + scale_attn_s), normed_one_s, inv_one_s
    )

    grad_mod_rows = jnp.concatenate(
        [
            grad_attn_in_s,
            grad_attn_in_s * normed_one_s,
            grad_mid_s * live_s * attn_out_s,
            grad_mlp_in_s,
            grad_mlp_in_s * normed_two_s,
            grad_result_s * live_s * mlp_out_s,
        ],
        axis=1,
    )
    grad_mod_share = jnp.dot(one_hot_s.T, grad_mod_rows, precision=lax.Precision.HIGHEST)
    piece_cols = mod_cols // n_dp
    pieces = jnp.transpose(
        grad_mod_share.reshape(latents, group, n_dp, piece_cols), (2, 1, 0, 3)
    ).reshape(n_dp * group, latents * piece_cols)
    own_piece = jnp.sum(lax.all_to_all(pieces, ALL, 0, 0), axis=0)
    small = jnp.concatenate(
        [
            own_piece,
            attn_b_part,
            jnp.sum(grad_pre, axis=0),
            jnp.sum(own_rows(grad_mlp), axis=0),
            jnp.sum(grad_attn_s, axis=0),
        ]
    )
    small_all = lax.all_gather(small, ALL, axis=0, tiled=False).reshape(n_dp, group, -1)
    small_own = lax.dynamic_index_in_dim(small_all, member, 1, keepdims=False)
    at = own_piece.shape[0]
    own_cols = jnp.transpose(
        small_own[:, :at].reshape(n_dp, latents, piece_cols), (1, 0, 2)
    ).reshape(latents, mod_cols)
    attn_b_own = small_own[:, at : at + 2 * HD].reshape(blocks, heads_here, 2, HD)
    attn_b_out = jnp.transpose(jnp.sum(attn_b_own, axis=0), (1, 0, 2)).reshape(2, columns)
    at = at + 2 * HD
    up_b_out = jnp.sum(small_own[:, at : at + hidden_cols], axis=0)
    at = at + hidden_cols
    both_b = jnp.sum(small_all[:, :, at:], axis=(0, 1))
    down_b_all, out_b_all = both_b[:width], both_b[width:]
    mod_w_out = jnp.dot(silu_own.astype(F32).T, own_cols, precision=lax.Precision.HIGHEST)
    mod_b_out = jnp.sum(own_cols, axis=0)
    silu_part = jnp.dot(own_cols, mod_weight.astype(F32).T, precision=lax.Precision.HIGHEST)
    silu_parts = lax.all_gather(silu_part, ALL, axis=0, tiled=False)
    silu_parts = jnp.sum(silu_parts.reshape(n_dp, group, latents, weight_rows), axis=1)
    grad_silu = jnp.transpose(silu_parts, (1, 0, 2)).reshape(latents, width)
    grad_conditioning = grad_silu * silu_slope(cond_vals)
    return (
        result_s,
        grad_tokens_s,
        grad_conditioning,
        attn_w_out,
        attn_b_out,
        out_w_out,
        out_b_all,
        up_w_out,
        up_b_out,
        down_w_out,
        down_b_all,
        mod_w_out,
        mod_b_out,
    )


def solution(mesh):
    n_dp = mesh.shape["dp"]
    fine = Mesh(mesh.devices.reshape(n_dp // BLOCK, BLOCK, mesh.shape["mp"]), ALL)
    placed = (
        P(DP, None),
        P(),
        P(DP),
        P(DP),
        P(None, DP, "mp"),
        P(None, "mp"),
        P("mp", DP),
        P(),
        P(DP, "mp"),
        P("mp"),
        P("mp", DP),
        P(),
        P(DP, "mp"),
        P("mp"),
        P(DP, None),
    )
    return jax.shard_map(
        shards,
        mesh=fine,
        in_specs=placed,
        out_specs=(
            P(ALL, None),
            P(ALL, None),
            P(),
            P(None, DP, "mp"),
            P(None, "mp"),
            P("mp", DP),
            P(),
            P(DP, "mp"),
            P("mp"),
            P("mp", DP),
            P(),
            P(DP, "mp"),
            P("mp"),
        ),
        check_vma=False,
    )
```

```python
import jax
import jax.numpy as jnp
from jax import lax
from jax.sharding import Mesh
from jax.sharding import PartitionSpec as P

HD = 72
KV_ROWS = 152
BLOCK = 4

EPSILON = 1e-06
NEG_FILL = -1e30
DP = ("da", "db")
ALL = ("da", "db", "mp")
BF = jnp.bfloat16
F32 = jnp.float32


def normalize(values):
    average = jnp.mean(values, axis=-1, keepdims=True)
    centered = values - average
    spread_sq = jnp.mean(centered * centered, axis=-1, keepdims=True)
    inv_std = lax.rsqrt(spread_sq + EPSILON)
    return (centered * inv_std, inv_std)


def normalize_back(grad_hat, normed, inv_std):
    first = jnp.mean(grad_hat, axis=-1, keepdims=True)
    second = jnp.mean(grad_hat * normed, axis=-1, keepdims=True)
    return inv_std * (grad_hat - first - normed * second)


def gelu_tanh(values):
    return jax.nn.gelu(values, approximate=True)


def silu_slope(values):
    sigma = jax.nn.sigmoid(values)
    return sigma * (1.0 + values * (1.0 - sigma))


def dot(left, right, left_dim, right_dim, **kw):
    return lax.dot_general(
        left, right, (((left_dim,), (right_dim,)), ((), ())), preferred_element_type=F32, **kw
    )


def scatter_rows(partial):
    rows, width = partial.shape
    member = lax.axis_index("mp")
    low, high = member % 2, member // 2
    halves = partial.reshape(2, 2, rows // 4, width)
    keep = lax.dynamic_index_in_dim(halves, low, 1, keepdims=False)
    give = lax.dynamic_index_in_dim(halves, 1 - low, 1, keepdims=False).astype(BF)
    kept = keep + lax.ppermute(give, "mp", [(m, m ^ 1) for m in range(4)]).astype(F32)
    keep = lax.dynamic_index_in_dim(kept, high, 0, keepdims=False)
    give = lax.dynamic_index_in_dim(kept, 1 - high, 0, keepdims=False).astype(BF)
    return keep + lax.ppermute(give, "mp", [(m, m ^ 2) for m in range(4)]).astype(F32)


def spread(values, axes, count):
    return lax.all_to_all(jnp.broadcast_to(values[None], (count,) + values.shape), axes, 0, 0)


def neighbours(block_kv, blocks):
    if blocks == 2:
        return [lax.ppermute(block_kv, "da", [(0, 1), (1, 0)])]
    return [
        lax.ppermute(block_kv, "da", [(i, i + 1) for i in range(blocks - 1)]),
        lax.ppermute(block_kv, "da", [(i + 1, i) for i in range(blocks - 1)]),
    ]


def return_grads(pieces, blocks):
    if blocks == 2:
        return lax.ppermute(pieces[0], "da", [(0, 1), (1, 0)]).astype(F32)
    return lax.ppermute(pieces[0], "da", [(i + 1, i) for i in range(blocks - 1)]).astype(
        F32
    ) + lax.ppermute(pieces[1], "da", [(i, i + 1) for i in range(blocks - 1)]).astype(F32)


def shards(
    tokens,
    conditioning,
    segments,
    live_counts,
    attn_weight,
    attn_bias,
    out_weight,
    out_bias,
    up_weight,
    up_bias,
    down_weight,
    down_bias,
    mod_weight,
    mod_bias,
    cotangent,
):
    tok_rows, width = tokens.shape
    latents = conditioning.shape[0]
    columns = attn_weight.shape[2]
    heads_here = columns // HD
    weight_rows = up_weight.shape[0]
    hidden_cols = up_bias.shape[0]
    mod_cols = mod_bias.shape[0]
    score_scale = 1.0 / HD**0.5
    blocks = lax.axis_size("da")
    group = lax.axis_size("mp")
    n_dp = blocks * BLOCK
    share = tok_rows // group
    member = lax.axis_index("mp")
    block_at = lax.axis_index("db")
    dp_at = lax.axis_index("da") * BLOCK + block_at
    row_start = member * share
    block_rows = BLOCK * tok_rows

    def own_rows(values):
        return lax.dynamic_slice_in_dim(values, row_start, share, 0)

    attn_local = jnp.transpose(
        attn_weight.reshape(3, weight_rows, heads_here, HD), (1, 2, 0, 3)
    )
    attn_local = attn_local[:, :, jnp.array([1, 2, 0])].reshape(weight_rows, 3 * columns)
    attn_and_out = lax.all_gather(
        jnp.concatenate([attn_local, out_weight.T], axis=1), DP, axis=0, tiled=True
    )
    attn_full, out_t = attn_and_out[:, : 3 * columns], attn_and_out[:, 3 * columns :]
    up_full = lax.all_gather(up_weight, DP, axis=0, tiled=True)
    down_t = lax.all_gather(down_weight.T, DP, axis=0, tiled=True)

    cond_vals = conditioning.astype(F32)
    silu_cond = jax.nn.silu(cond_vals).astype(BF)
    silu_own = lax.dynamic_slice_in_dim(silu_cond, dp_at * weight_rows, weight_rows, 1)
    mod_part = dot(silu_own, mod_weight, 1, 0)
    mod_part = mod_part + jnp.where(dp_at == 0, 1.0, 0.0) * mod_bias
    piece_cols = mod_cols // n_dp
    mod_pieces = jnp.transpose(mod_part.reshape(latents, n_dp, piece_cols), (1, 0, 2))
    mod_piece = jnp.sum(
        lax.all_to_all(mod_pieces.reshape(n_dp, latents * piece_cols), DP, 0, 0), axis=0
    )
    modulation = spread(mod_piece, ALL, n_dp * group).reshape(n_dp, group, latents, piece_cols)
    modulation = jnp.transpose(modulation, (2, 1, 0, 3)).reshape(latents, 6 * width)
    one_hot = (segments[:, None] == jnp.arange(latents, dtype=jnp.int32)[None, :]).astype(F32)
    one_hot_s = own_rows(one_hot)

    def modulate(hot, first, last):
        return jnp.dot(
            hot, modulation[:, first * width : last * width], precision=lax.Precision.HIGHEST
        )

    shift_attn, scale_attn = jnp.split(modulate(one_hot, 0, 2), 2, axis=1)
    gate_mlp = modulate(one_hot, 5, 6)
    scale_attn_s, gate_attn_s, shift_mlp_s, scale_mlp_s, gate_mlp_s = jnp.split(
        modulate(one_hot_s, 1, 6), 5, axis=1
    )
    live = (jnp.arange(tok_rows, dtype=jnp.int32) < live_counts[0]).astype(F32)[:, None]
    live_s = own_rows(live)
    token_vals = tokens.astype(F32)
    token_s = own_rows(token_vals)
    normed_one, inv_one = normalize(token_vals)
    attn_input = (normed_one * (1.0 + scale_attn) + shift_attn).astype(BF)

    head_bias = attn_bias.reshape(2, heads_here, HD)
    bias_t = jnp.stack([jnp.zeros_like(head_bias[0]), head_bias[1], head_bias[0]], axis=1)
    kvq_t = (dot(attn_full, attn_input, 0, 1) + bias_t.reshape(3 * columns)[:, None]).astype(BF)
    kvq_t = kvq_t.reshape(heads_here, 3 * HD, tok_rows)
    tags = jnp.stack(
        [jnp.where(live[:, 0] > 0.0, segments + 1, 0).astype(BF), (segments + 1).astype(BF)]
    )
    tags = jnp.pad(tags, ((0, KV_ROWS - 2 * HD - 2), (0, 0)))
    tags = jnp.broadcast_to(tags[None], (heads_here,) + tags.shape)
    sent = jnp.concatenate([kvq_t[:, : 2 * HD], tags, kvq_t[:, 2 * HD :]], axis=1)
    got = lax.all_to_all(sent, "db", 0, 0)
    kv_own = got[:, :KV_ROWS]
    kv_all = jnp.stack([kv_own] + neighbours(kv_own, blocks))
    key_blocks = kv_all.shape[0]
    keys_seen = key_blocks * block_rows
    kv_t = jnp.transpose(kv_all, (2, 0, 1, 3)).reshape(KV_ROWS, keys_seen)
    key_t, value_t = kv_t[:HD], kv_t[HD : 2 * HD]
    key_tag = kv_t[2 * HD].astype(F32)
    query_tag = kv_t[2 * HD + 1, :block_rows].astype(F32)
    query_t = jnp.transpose(got[:, KV_ROWS:], (1, 0, 2)).reshape(HD, block_rows)
    self_mask = (
        jnp.arange(keys_seen, dtype=jnp.int32)[None, :]
        == jnp.arange(block_rows, dtype=jnp.int32)[:, None]
    )
    allowed = (key_tag[None, :] == query_tag[:, None]) | self_mask

    def masked_scores():
        return jnp.where(allowed, dot(query_t, key_t, 0, 0) * score_scale, NEG_FILL)

    scores = masked_scores()
    row_max = jnp.max(scores, axis=-1, keepdims=True)
    log_total = row_max + jnp.log(jnp.sum(jnp.exp(scores - row_max), axis=-1, keepdims=True))
    attn_exact = jnp.exp(scores - log_total)
    attn_probs = attn_exact.astype(BF)
    head_attended = dot(value_t, attn_probs, 1, 1).astype(BF)

    def to_owners(head_rows):
        rows = head_rows.shape[0]
        parts = jnp.transpose(head_rows.reshape(rows, BLOCK, tok_rows), (1, 0, 2))
        return lax.all_to_all(parts, "db", 0, 0).reshape(heads_here * rows, tok_rows)

    attended_t = to_owners(head_attended)
    attn_out_s = scatter_rows(dot(attended_t, out_t, 0, 1)) + out_bias
    mid_s = token_s + live_s * gate_attn_s * attn_out_s
    normed_two_s, inv_two_s = normalize(mid_s)
    mlp_input_s = (normed_two_s * (1.0 + scale_mlp_s) + shift_mlp_s).astype(BF)
    mlp_input = lax.all_gather(mlp_input_s, "mp", axis=0, tiled=True)
    hidden_pre = dot(mlp_input, up_full, 1, 0) + up_bias
    hidden = gelu_tanh(hidden_pre).astype(BF)

    grad_result = cotangent.astype(F32)
    grad_result_s = own_rows(grad_result)
    grad_mlp = grad_result * live * gate_mlp
    grad_mlp_b = grad_mlp.astype(BF)
    grad_hidden = dot(grad_mlp_b, down_t, 1, 0)
    grad_pre = jax.vjp(gelu_tanh, hidden_pre)[1](grad_hidden)[0]
    grad_pre_b = grad_pre.astype(BF)
    grad_mlp_in_s = scatter_rows(dot(grad_pre_b, up_full, 1, 1))
    grad_mid_s = grad_result_s + normalize_back(
        grad_mlp_in_s * (1.0 + scale_mlp_s), normed_two_s, inv_two_s
    )
    grad_attn_s = grad_mid_s * live_s * gate_attn_s
    grad_attn_b = lax.all_gather(grad_attn_s.astype(BF), "mp", axis=0, tiled=True)
    grad_down_w = dot(grad_mlp_b, hidden, 0, 0)
    grad_up_w = dot(mlp_input, grad_pre_b, 0, 0)
    mlp_w = lax.psum_scatter(
        jnp.concatenate([grad_up_w.astype(BF), grad_down_w.astype(BF)], axis=1),
        DP,
        scatter_dimension=0,
        tiled=True,
    )
    mlp_out_s = scatter_rows(dot(hidden, down_t, 1, 1)) + down_bias
    result_s = (mid_s + live_s * gate_mlp_s * mlp_out_s).astype(BF)

    grad_attended_t = dot(out_t, grad_attn_b, 0, 1).astype(BF)
    got_grad = lax.all_to_all(grad_attended_t.reshape(heads_here, HD, tok_rows), "db", 0, 0)
    grad_t = jnp.transpose(got_grad, (1, 0, 2)).reshape(HD, block_rows)
    grad_probs = dot(grad_t, value_t, 0, 0)
    delta = jnp.sum(grad_t.astype(F32) * head_attended.astype(F32), axis=0)[:, None]
    grad_scores = (attn_exact * (grad_probs - delta)).astype(BF)
    grad_query_t = dot(key_t, grad_scores, 1, 1) * score_scale
    grad_key_t = dot(query_t, grad_scores, 1, 0) * score_scale
    grad_value_t = dot(grad_t, attn_probs, 1, 0)
    grad_kv_t = jnp.concatenate([grad_key_t, grad_value_t])
    others = [
        grad_kv_t[:, i * block_rows : (i + 1) * block_rows].astype(BF)
        for i in range(1, key_blocks)
    ]
    grad_kv_own = grad_kv_t[:, :block_rows] + return_grads(others, blocks)
    attn_b_part = jnp.concatenate(
        [jnp.sum(grad_query_t, axis=1), jnp.sum(grad_kv_own[HD:], axis=1)]
    )
    grad_kvq_t = to_owners(jnp.concatenate([grad_kv_own, grad_query_t]).astype(BF))
    grad_attn_w = dot(attn_input, grad_kvq_t, 0, 1)
    grad_out_w = dot(grad_attn_b, attended_t, 0, 1)
    late_terms, mlp_w = lax.optimization_barrier(
        (jnp.concatenate([grad_attn_w.astype(BF), grad_out_w.astype(BF)], axis=1), mlp_w)
    )
    up_w_out, down_w_out = mlp_w[:, :hidden_cols].astype(F32), mlp_w[:, hidden_cols:].T.astype(F32)
    attn_w = lax.psum_scatter(late_terms, DP, scatter_dimension=0, tiled=True).astype(F32)
    out_w_out = attn_w[:, 3 * columns :].T
    attn_w_out = attn_w[:, : 3 * columns].reshape(weight_rows, heads_here, 3, HD)
    attn_w_out = jnp.transpose(attn_w_out[:, :, jnp.array([2, 0, 1])], (2, 0, 1, 3)).reshape(
        3, weight_rows, columns
    )
    grad_attn_in_s = scatter_rows(dot(grad_kvq_t, attn_full, 0, 1))
    normed_one_s = own_rows(normed_one)
    inv_one_s = own_rows(inv_one)
    grad_tokens_s = grad_mid_s + normalize_back(
        grad_attn_in_s * (1.0 + scale_attn_s), normed_one_s, inv_one_s
    )

    grad_mod_rows = jnp.concatenate(
        [
            grad_attn_in_s,
            grad_attn_in_s * normed_one_s,
            grad_mid_s * live_s * attn_out_s,
            grad_mlp_in_s,
            grad_mlp_in_s * normed_two_s,
            grad_result_s * live_s * mlp_out_s,
        ],
        axis=1,
    )
    grad_mod_share = jnp.dot(one_hot_s.T, grad_mod_rows, precision=lax.Precision.HIGHEST)
    pieces = jnp.transpose(
        grad_mod_share.reshape(latents, group, n_dp, piece_cols), (2, 1, 0, 3)
    ).reshape(n_dp * group, latents * piece_cols)
    own_piece = jnp.sum(lax.all_to_all(pieces, ALL, 0, 0), axis=0)
    small = jnp.concatenate(
        [
            own_piece,
            attn_b_part,
            jnp.sum(grad_pre, axis=0),
            jnp.sum(own_rows(grad_mlp), axis=0),
            jnp.sum(grad_attn_s, axis=0),
        ]
    )
    small_all = spread(small, ALL, n_dp * group).reshape(n_dp, group, -1)
    small_own = lax.dynamic_index_in_dim(small_all, member, 1, keepdims=False)
    at = own_piece.shape[0]
    own_cols = jnp.transpose(
        small_own[:, :at].reshape(n_dp, latents, piece_cols), (1, 0, 2)
    ).reshape(latents, mod_cols)
    attn_b_own = small_own[:, at : at + 2 * HD].reshape(blocks, heads_here, 2, HD)
    attn_b_out = jnp.transpose(jnp.sum(attn_b_own, axis=0), (1, 0, 2)).reshape(2, columns)
    at = at + 2 * HD
    up_b_out = jnp.sum(small_own[:, at : at + hidden_cols], axis=0)
    at = at + hidden_cols
    both_b = jnp.sum(small_all[:, :, at:], axis=(0, 1))
    down_b_all, out_b_all = both_b[:width], both_b[width:]
    mod_w_out = jnp.dot(silu_own.astype(F32).T, own_cols, precision=lax.Precision.HIGHEST)
    mod_b_out = jnp.sum(own_cols, axis=0)
    silu_part = jnp.dot(own_cols, mod_weight.astype(F32).T, precision=lax.Precision.HIGHEST)
    silu_parts = spread(silu_part.reshape(-1), ALL, n_dp * group)
    silu_parts = jnp.sum(silu_parts.reshape(n_dp, group, latents, weight_rows), axis=1)
    grad_silu = jnp.transpose(silu_parts, (1, 0, 2)).reshape(latents, width)
    grad_conditioning = grad_silu * silu_slope(cond_vals)
    return (
        result_s,
        grad_tokens_s,
        grad_conditioning,
        attn_w_out,
        attn_b_out,
        out_w_out,
        out_b_all,
        up_w_out,
        up_b_out,
        down_w_out,
        down_b_all,
        mod_w_out,
        mod_b_out,
    )


def solution(mesh):
    n_dp = mesh.shape["dp"]
    fine = Mesh(mesh.devices.reshape(n_dp // BLOCK, BLOCK, mesh.shape["mp"]), ALL)
    placed = (
        P(DP, None),
        P(),
        P(DP),
        P(DP),
        P(None, DP, "mp"),
        P(None, "mp"),
        P("mp", DP),
        P(),
        P(DP, "mp"),
        P("mp"),
        P("mp", DP),
        P(),
        P(DP, "mp"),
        P("mp"),
        P(DP, None),
    )
    return jax.shard_map(
        shards,
        mesh=fine,
        in_specs=placed,
        out_specs=(
            P(ALL, None),
            P(ALL, None),
            P(),
            P(None, DP, "mp"),
            P(None, "mp"),
            P("mp", DP),
            P(),
            P(DP, "mp"),
            P("mp"),
            P("mp", DP),
            P(),
            P(DP, "mp"),
            P("mp"),
        ),
        check_vma=False,
    )
```

```python
import jax
import jax.numpy as jnp
from jax import lax
from jax.sharding import Mesh
from jax.sharding import PartitionSpec as P

HD = 72
KV_ROWS = 152
BLOCK = 4

EPSILON = 1e-06
NEG_FILL = -1e30
DP = ("da", "db")
ALL = ("da", "db", "mp")
BF = jnp.bfloat16
F32 = jnp.float32


def normalize(values):
    average = jnp.mean(values, axis=-1, keepdims=True)
    centered = values - average
    spread_sq = jnp.mean(centered * centered, axis=-1, keepdims=True)
    inv_std = lax.rsqrt(spread_sq + EPSILON)
    return (centered * inv_std, inv_std)


def normalize_back(grad_hat, normed, inv_std):
    first = jnp.mean(grad_hat, axis=-1, keepdims=True)
    second = jnp.mean(grad_hat * normed, axis=-1, keepdims=True)
    return inv_std * (grad_hat - first - normed * second)


def gelu_tanh(values):
    return jax.nn.gelu(values, approximate=True)


def silu_slope(values):
    sigma = jax.nn.sigmoid(values)
    return sigma * (1.0 + values * (1.0 - sigma))


def dot(left, right, left_dim, right_dim, **kw):
    return lax.dot_general(
        left, right, (((left_dim,), (right_dim,)), ((), ())), preferred_element_type=F32, **kw
    )


def scatter_rows(partial):
    rows, width = partial.shape
    member = lax.axis_index("mp")
    low, high = member % 2, member // 2
    halves = partial.reshape(2, 2, rows // 4, width)
    keep = lax.dynamic_index_in_dim(halves, low, 1, keepdims=False)
    give = lax.dynamic_index_in_dim(halves, 1 - low, 1, keepdims=False).astype(BF)
    kept = keep + lax.ppermute(give, "mp", [(m, m ^ 1) for m in range(4)]).astype(F32)
    keep = lax.dynamic_index_in_dim(kept, high, 0, keepdims=False)
    give = lax.dynamic_index_in_dim(kept, 1 - high, 0, keepdims=False).astype(BF)
    return keep + lax.ppermute(give, "mp", [(m, m ^ 2) for m in range(4)]).astype(F32)


def spread(values, axes, count):
    return lax.all_to_all(jnp.broadcast_to(values[None], (count,) + values.shape), axes, 0, 0)


def neighbours(block_kv, blocks):
    if blocks == 2:
        return [lax.ppermute(block_kv, "da", [(0, 1), (1, 0)])]
    return [
        lax.ppermute(block_kv, "da", [(i, i + 1) for i in range(blocks - 1)]),
        lax.ppermute(block_kv, "da", [(i + 1, i) for i in range(blocks - 1)]),
    ]


def return_grads(pieces, blocks):
    if blocks == 2:
        return lax.ppermute(pieces[0], "da", [(0, 1), (1, 0)]).astype(F32)
    return lax.ppermute(pieces[0], "da", [(i + 1, i) for i in range(blocks - 1)]).astype(
        F32
    ) + lax.ppermute(pieces[1], "da", [(i, i + 1) for i in range(blocks - 1)]).astype(F32)


def shards(
    tokens,
    conditioning,
    segments,
    live_counts,
    attn_weight,
    attn_bias,
    out_weight,
    out_bias,
    up_weight,
    up_bias,
    down_weight,
    down_bias,
    mod_weight,
    mod_bias,
    cotangent,
):
    tok_rows, width = tokens.shape
    latents = conditioning.shape[0]
    columns = attn_weight.shape[2]
    heads_here = columns // HD
    weight_rows = up_weight.shape[0]
    hidden_cols = up_bias.shape[0]
    mod_cols = mod_bias.shape[0]
    score_scale = 1.0 / HD**0.5
    blocks = lax.axis_size("da")
    group = lax.axis_size("mp")
    n_dp = blocks * BLOCK
    share = tok_rows // group
    member = lax.axis_index("mp")
    block_at = lax.axis_index("db")
    dp_at = lax.axis_index("da") * BLOCK + block_at
    row_start = member * share
    block_rows = BLOCK * tok_rows

    def own_rows(values):
        return lax.dynamic_slice_in_dim(values, row_start, share, 0)

    attn_local = jnp.transpose(
        attn_weight.reshape(3, weight_rows, heads_here, HD), (1, 2, 0, 3)
    )
    attn_local = attn_local[:, :, jnp.array([1, 2, 0])].reshape(weight_rows, 3 * columns)
    attn_and_out = lax.all_gather(
        jnp.concatenate([attn_local, out_weight.T], axis=1), DP, axis=0, tiled=True
    )
    attn_full, out_t = attn_and_out[:, : 3 * columns], attn_and_out[:, 3 * columns :]
    up_and_down = lax.all_gather(
        jnp.concatenate([up_weight, down_weight.T], axis=1), DP, axis=0, tiled=True
    )
    up_full, down_t = up_and_down[:, :hidden_cols], up_and_down[:, hidden_cols:]

    cond_vals = conditioning.astype(F32)
    silu_cond = jax.nn.silu(cond_vals).astype(BF)
    silu_own = lax.dynamic_slice_in_dim(silu_cond, dp_at * weight_rows, weight_rows, 1)
    mod_part = dot(silu_own, mod_weight, 1, 0)
    mod_part = mod_part + jnp.where(dp_at == 0, 1.0, 0.0) * mod_bias
    piece_cols = mod_cols // n_dp
    mod_pieces = jnp.transpose(mod_part.reshape(latents, n_dp, piece_cols), (1, 0, 2))
    mod_piece = jnp.sum(
        lax.all_to_all(mod_pieces.reshape(n_dp, latents * piece_cols), DP, 0, 0), axis=0
    )
    modulation = spread(mod_piece, ALL, n_dp * group).reshape(n_dp, group, latents, piece_cols)
    modulation = jnp.transpose(modulation, (2, 1, 0, 3)).reshape(latents, 6 * width)
    one_hot = (segments[:, None] == jnp.arange(latents, dtype=jnp.int32)[None, :]).astype(F32)
    one_hot_s = own_rows(one_hot)

    def modulate(hot, first, last):
        return jnp.dot(
            hot, modulation[:, first * width : last * width], precision=lax.Precision.HIGHEST
        )

    shift_attn, scale_attn = jnp.split(modulate(one_hot, 0, 2), 2, axis=1)
    gate_mlp = modulate(one_hot, 5, 6)
    scale_attn_s, gate_attn_s, shift_mlp_s, scale_mlp_s, gate_mlp_s = jnp.split(
        modulate(one_hot_s, 1, 6), 5, axis=1
    )
    live = (jnp.arange(tok_rows, dtype=jnp.int32) < live_counts[0]).astype(F32)[:, None]
    live_s = own_rows(live)
    token_vals = tokens.astype(F32)
    token_s = own_rows(token_vals)
    normed_one, inv_one = normalize(token_vals)
    attn_input = (normed_one * (1.0 + scale_attn) + shift_attn).astype(BF)

    head_bias = attn_bias.reshape(2, heads_here, HD)
    bias_t = jnp.stack([jnp.zeros_like(head_bias[0]), head_bias[1], head_bias[0]], axis=1)
    kvq_t = (dot(attn_full, attn_input, 0, 1) + bias_t.reshape(3 * columns)[:, None]).astype(BF)
    kvq_t = kvq_t.reshape(heads_here, 3 * HD, tok_rows)
    tags = jnp.stack(
        [jnp.where(live[:, 0] > 0.0, segments + 1, 0).astype(BF), (segments + 1).astype(BF)]
    )
    tags = jnp.pad(tags, ((0, KV_ROWS - 2 * HD - 2), (0, 0)))
    tags = jnp.broadcast_to(tags[None], (heads_here,) + tags.shape)
    sent = jnp.concatenate([kvq_t[:, : 2 * HD], tags, kvq_t[:, 2 * HD :]], axis=1)
    got = lax.all_to_all(sent, "db", 0, 0)
    kv_own = got[:, :KV_ROWS]
    kv_all = jnp.stack([kv_own] + neighbours(kv_own, blocks))
    key_blocks = kv_all.shape[0]
    keys_seen = key_blocks * block_rows
    kv_t = jnp.transpose(kv_all, (2, 0, 1, 3)).reshape(KV_ROWS, keys_seen)
    key_t, value_t = kv_t[:HD], kv_t[HD : 2 * HD]
    key_tag = kv_t[2 * HD].astype(F32)
    query_tag = kv_t[2 * HD + 1, :block_rows].astype(F32)
    query_t = jnp.transpose(got[:, KV_ROWS:], (1, 0, 2)).reshape(HD, block_rows)
    self_mask = (
        jnp.arange(keys_seen, dtype=jnp.int32)[None, :]
        == jnp.arange(block_rows, dtype=jnp.int32)[:, None]
    )
    allowed = (key_tag[None, :] == query_tag[:, None]) | self_mask

    def masked_scores():
        return jnp.where(allowed, dot(query_t, key_t, 0, 0) * score_scale, NEG_FILL)

    scores = masked_scores()
    row_max = jnp.max(scores, axis=-1, keepdims=True)
    log_total = row_max + jnp.log(jnp.sum(jnp.exp(scores - row_max), axis=-1, keepdims=True))
    attn_exact = jnp.exp(scores - log_total)
    attn_probs = attn_exact.astype(BF)
    head_attended = dot(value_t, attn_probs, 1, 1).astype(BF)

    def to_owners(head_rows):
        rows = head_rows.shape[0]
        parts = jnp.transpose(head_rows.reshape(rows, BLOCK, tok_rows), (1, 0, 2))
        return lax.all_to_all(parts, "db", 0, 0).reshape(heads_here * rows, tok_rows)

    attended_t = to_owners(head_attended)
    attn_out_s = scatter_rows(dot(attended_t, out_t, 0, 1)) + out_bias
    mid_s = token_s + live_s * gate_attn_s * attn_out_s
    normed_two_s, inv_two_s = normalize(mid_s)
    mlp_input_s = (normed_two_s * (1.0 + scale_mlp_s) + shift_mlp_s).astype(BF)
    mlp_input = lax.all_gather(mlp_input_s, "mp", axis=0, tiled=True)
    hidden_pre = dot(mlp_input, up_full, 1, 0) + up_bias
    hidden = gelu_tanh(hidden_pre).astype(BF)

    grad_result = cotangent.astype(F32)
    grad_result_s = own_rows(grad_result)
    grad_mlp = grad_result * live * gate_mlp
    grad_mlp_b = grad_mlp.astype(BF)
    grad_hidden = dot(grad_mlp_b, down_t, 1, 0)
    grad_pre = jax.vjp(gelu_tanh, hidden_pre)[1](grad_hidden)[0]
    grad_pre_b = grad_pre.astype(BF)
    grad_mlp_in_s = scatter_rows(dot(grad_pre_b, up_full, 1, 1))
    grad_mid_s = grad_result_s + normalize_back(
        grad_mlp_in_s * (1.0 + scale_mlp_s), normed_two_s, inv_two_s
    )
    grad_attn_s = grad_mid_s * live_s * gate_attn_s
    grad_attn_b = lax.all_gather(grad_attn_s.astype(BF), "mp", axis=0, tiled=True)
    grad_down_w = dot(grad_mlp_b, hidden, 0, 0)
    grad_up_w = dot(mlp_input, grad_pre_b, 0, 0)
    mlp_w = lax.psum_scatter(
        jnp.concatenate([grad_up_w.astype(BF), grad_down_w.astype(BF)], axis=1),
        DP,
        scatter_dimension=0,
        tiled=True,
    )
    mlp_out_s = scatter_rows(dot(hidden, down_t, 1, 1)) + down_bias
    result_s = (mid_s + live_s * gate_mlp_s * mlp_out_s).astype(BF)

    grad_attended_t = dot(out_t, grad_attn_b, 0, 1).astype(BF)
    got_grad = lax.all_to_all(grad_attended_t.reshape(heads_here, HD, tok_rows), "db", 0, 0)
    grad_t = jnp.transpose(got_grad, (1, 0, 2)).reshape(HD, block_rows)
    grad_probs = dot(grad_t, value_t, 0, 0)
    delta = jnp.sum(grad_t.astype(F32) * head_attended.astype(F32), axis=0)[:, None]
    grad_scores = (attn_exact * (grad_probs - delta)).astype(BF)
    grad_query_t = dot(key_t, grad_scores, 1, 1) * score_scale
    grad_key_t = dot(query_t, grad_scores, 1, 0) * score_scale
    grad_value_t = dot(grad_t, attn_probs, 1, 0)
    grad_kv_t = jnp.concatenate([grad_key_t, grad_value_t])
    others = [
        grad_kv_t[:, i * block_rows : (i + 1) * block_rows].astype(BF)
        for i in range(1, key_blocks)
    ]
    grad_kv_own = grad_kv_t[:, :block_rows] + return_grads(others, blocks)
    attn_b_part = jnp.concatenate(
        [jnp.sum(grad_query_t, axis=1), jnp.sum(grad_kv_own[HD:], axis=1)]
    )
    grad_kvq_t = to_owners(jnp.concatenate([grad_kv_own, grad_query_t]).astype(BF))
    grad_attn_w = dot(attn_input, grad_kvq_t, 0, 1)
    grad_out_w = dot(grad_attn_b, attended_t, 0, 1)
    attn_terms, mlp_w = lax.optimization_barrier((grad_attn_w.astype(BF), mlp_w))
    up_w_out, down_w_out = mlp_w[:, :hidden_cols].astype(F32), mlp_w[:, hidden_cols:].T.astype(F32)
    pieces = grad_out_w.astype(BF).reshape(n_dp, weight_rows, columns)
    out_w_out = jnp.sum(lax.all_to_all(pieces, DP, 0, 0).astype(F32), axis=0).T
    attn_w = lax.psum_scatter(attn_terms, DP, scatter_dimension=0, tiled=True).astype(F32)
    attn_w_out = attn_w.reshape(weight_rows, heads_here, 3, HD)
    attn_w_out = jnp.transpose(attn_w_out[:, :, jnp.array([2, 0, 1])], (2, 0, 1, 3)).reshape(
        3, weight_rows, columns
    )
    grad_attn_in_s = scatter_rows(dot(grad_kvq_t, attn_full, 0, 1))
    normed_one_s = own_rows(normed_one)
    inv_one_s = own_rows(inv_one)
    grad_tokens_s = grad_mid_s + normalize_back(
        grad_attn_in_s * (1.0 + scale_attn_s), normed_one_s, inv_one_s
    )

    grad_mod_rows = jnp.concatenate(
        [
            grad_attn_in_s,
            grad_attn_in_s * normed_one_s,
            grad_mid_s * live_s * attn_out_s,
            grad_mlp_in_s,
            grad_mlp_in_s * normed_two_s,
            grad_result_s * live_s * mlp_out_s,
        ],
        axis=1,
    )
    grad_mod_share = jnp.dot(one_hot_s.T, grad_mod_rows, precision=lax.Precision.HIGHEST)
    pieces = jnp.transpose(
        grad_mod_share.reshape(latents, group, n_dp, piece_cols), (2, 1, 0, 3)
    ).reshape(n_dp * group, latents * piece_cols)
    up_piece = jnp.repeat(jnp.sum(grad_pre, axis=0).reshape(n_dp, -1), group, axis=0)
    both_part = jnp.concatenate([jnp.sum(own_rows(grad_mlp), axis=0), jnp.sum(grad_attn_s, axis=0)])
    both_piece = both_part.reshape(n_dp * group, -1)
    taken = lax.all_to_all(
        jnp.concatenate([pieces, both_piece, up_piece], axis=1), ALL, 0, 0
    )
    at = latents * piece_cols
    both_at = at + both_piece.shape[1]
    from_group = taken[:, both_at:].reshape(n_dp, group, -1)
    up_sum = jnp.sum(lax.dynamic_index_in_dim(from_group, member, 1, keepdims=False), axis=0)
    small = jnp.concatenate([jnp.sum(taken[:, :both_at], axis=0), up_sum, attn_b_part])
    small_all = spread(small, ALL, n_dp * group).reshape(n_dp, group, -1)
    small_own = lax.dynamic_index_in_dim(small_all, member, 1, keepdims=False)
    own_cols = jnp.transpose(
        small_own[:, :at].reshape(n_dp, latents, piece_cols), (1, 0, 2)
    ).reshape(latents, mod_cols)
    both_b = small_all[:, :, at:both_at].reshape(2 * width)
    down_b_all, out_b_all = both_b[:width], both_b[width:]
    up_at = both_at + up_sum.shape[0]
    up_b_out = small_own[:, both_at:up_at].reshape(hidden_cols)
    attn_b_own = small_own[:, up_at:].reshape(blocks, heads_here, 2, HD)
    attn_b_out = jnp.transpose(jnp.sum(attn_b_own, axis=0), (1, 0, 2)).reshape(2, columns)
    mod_w_out = jnp.dot(silu_own.astype(F32).T, own_cols, precision=lax.Precision.HIGHEST)
    mod_b_out = jnp.sum(own_cols, axis=0)
    silu_part = jnp.dot(own_cols, mod_weight.astype(F32).T, precision=lax.Precision.HIGHEST)
    silu_parts = spread(silu_part.reshape(-1), ALL, n_dp * group)
    silu_parts = jnp.sum(silu_parts.reshape(n_dp, group, latents, weight_rows), axis=1)
    grad_silu = jnp.transpose(silu_parts, (1, 0, 2)).reshape(latents, width)
    grad_conditioning = grad_silu * silu_slope(cond_vals)
    return (
        result_s,
        grad_tokens_s,
        grad_conditioning,
        attn_w_out,
        attn_b_out,
        out_w_out,
        out_b_all,
        up_w_out,
        up_b_out,
        down_w_out,
        down_b_all,
        mod_w_out,
        mod_b_out,
    )


def solution(mesh):
    n_dp = mesh.shape["dp"]
    fine = Mesh(mesh.devices.reshape(n_dp // BLOCK, BLOCK, mesh.shape["mp"]), ALL)
    placed = (
        P(DP, None),
        P(),
        P(DP),
        P(DP),
        P(None, DP, "mp"),
        P(None, "mp"),
        P("mp", DP),
        P(),
        P(DP, "mp"),
        P("mp"),
        P("mp", DP),
        P(),
        P(DP, "mp"),
        P("mp"),
        P(DP, None),
    )
    return jax.shard_map(
        shards,
        mesh=fine,
        in_specs=placed,
        out_specs=(
            P(ALL, None),
            P(ALL, None),
            P(),
            P(None, DP, "mp"),
            P(None, "mp"),
            P("mp", DP),
            P(),
            P(DP, "mp"),
            P("mp"),
            P("mp", DP),
            P(),
            P(DP, "mp"),
            P("mp"),
        ),
        check_vma=False,
    )
```

```python
import jax
import jax.numpy as jnp
from jax import lax
from jax.sharding import Mesh
from jax.sharding import PartitionSpec as P

HD = 72
KV_ROWS = 152
BLOCK = 4

EPSILON = 1e-06
NEG_FILL = -1e30
DP = ("da", "db")
ALL = ("da", "db", "mp")
BF = jnp.bfloat16
F32 = jnp.float32


def normalize(values):
    average = jnp.mean(values, axis=-1, keepdims=True)
    centered = values - average
    spread_sq = jnp.mean(centered * centered, axis=-1, keepdims=True)
    inv_std = lax.rsqrt(spread_sq + EPSILON)
    return (centered * inv_std, inv_std)


def normalize_back(grad_hat, normed, inv_std):
    first = jnp.mean(grad_hat, axis=-1, keepdims=True)
    second = jnp.mean(grad_hat * normed, axis=-1, keepdims=True)
    return inv_std * (grad_hat - first - normed * second)


def gelu_tanh(values):
    return jax.nn.gelu(values, approximate=True)


def silu_slope(values):
    sigma = jax.nn.sigmoid(values)
    return sigma * (1.0 + values * (1.0 - sigma))


def dot(left, right, left_dim, right_dim, **kw):
    return lax.dot_general(
        left, right, (((left_dim,), (right_dim,)), ((), ())), preferred_element_type=F32, **kw
    )


def scatter_rows(partial):
    rows, width = partial.shape
    member = lax.axis_index("mp")
    low, high = member % 2, member // 2
    halves = partial.reshape(2, 2, rows // 4, width)
    keep = lax.dynamic_index_in_dim(halves, low, 1, keepdims=False)
    give = lax.dynamic_index_in_dim(halves, 1 - low, 1, keepdims=False).astype(BF)
    kept = keep + lax.ppermute(give, "mp", [(m, m ^ 1) for m in range(4)]).astype(F32)
    keep = lax.dynamic_index_in_dim(kept, high, 0, keepdims=False)
    give = lax.dynamic_index_in_dim(kept, 1 - high, 0, keepdims=False).astype(BF)
    return keep + lax.ppermute(give, "mp", [(m, m ^ 2) for m in range(4)]).astype(F32)


def spread(values, axes, count):
    return lax.all_to_all(jnp.broadcast_to(values[None], (count,) + values.shape), axes, 0, 0)


def doubled(rows, axis, bit):
    got = lax.ppermute(rows, axis, [(i, i ^ bit) for i in range(4)])
    low = (lax.axis_index(axis) & bit) == 0
    return jnp.concatenate([jnp.where(low, rows, got), jnp.where(low, got, rows)])


def neighbours(block_kv, blocks):
    if blocks == 2:
        return [lax.ppermute(block_kv, "da", [(0, 1), (1, 0)])]
    return [
        lax.ppermute(block_kv, "da", [(i, i + 1) for i in range(blocks - 1)]),
        lax.ppermute(block_kv, "da", [(i + 1, i) for i in range(blocks - 1)]),
    ]


def return_grads(pieces, blocks):
    if blocks == 2:
        return lax.ppermute(pieces[0], "da", [(0, 1), (1, 0)]).astype(F32)
    return lax.ppermute(pieces[0], "da", [(i + 1, i) for i in range(blocks - 1)]).astype(
        F32
    ) + lax.ppermute(pieces[1], "da", [(i, i + 1) for i in range(blocks - 1)]).astype(F32)


def shards(
    tokens,
    conditioning,
    segments,
    live_counts,
    attn_weight,
    attn_bias,
    out_weight,
    out_bias,
    up_weight,
    up_bias,
    down_weight,
    down_bias,
    mod_weight,
    mod_bias,
    cotangent,
):
    tok_rows, width = tokens.shape
    latents = conditioning.shape[0]
    columns = attn_weight.shape[2]
    heads_here = columns // HD
    weight_rows = up_weight.shape[0]
    hidden_cols = up_bias.shape[0]
    mod_cols = mod_bias.shape[0]
    score_scale = 1.0 / HD**0.5
    blocks = lax.axis_size("da")
    group = lax.axis_size("mp")
    n_dp = blocks * BLOCK
    share = tok_rows // group
    member = lax.axis_index("mp")
    block_at = lax.axis_index("db")
    dp_at = lax.axis_index("da") * BLOCK + block_at
    row_start = member * share
    block_rows = BLOCK * tok_rows

    def own_rows(values):
        return lax.dynamic_slice_in_dim(values, row_start, share, 0)

    attn_local = jnp.transpose(
        attn_weight.reshape(3, weight_rows, heads_here, HD), (1, 2, 0, 3)
    )
    attn_local = jnp.concatenate([attn_local[:, :, 1:], attn_local[:, :, :1]], axis=2).reshape(
        weight_rows, 3 * columns
    )
    attn_and_out = lax.all_gather(
        jnp.concatenate([attn_local, out_weight.T], axis=1), DP, axis=0, tiled=True
    )
    attn_full, out_t = attn_and_out[:, : 3 * columns], attn_and_out[:, 3 * columns :]
    up_and_down = lax.all_gather(
        jnp.concatenate([up_weight, down_weight.T], axis=1), DP, axis=0, tiled=True
    )
    up_full, down_t = up_and_down[:, :hidden_cols], up_and_down[:, hidden_cols:]

    cond_vals = conditioning.astype(F32)
    silu_cond = jax.nn.silu(cond_vals).astype(BF)
    silu_own = lax.dynamic_slice_in_dim(silu_cond, dp_at * weight_rows, weight_rows, 1)
    mod_part = dot(silu_own, mod_weight, 1, 0)
    mod_part = mod_part + jnp.where(dp_at == 0, 1.0, 0.0) * mod_bias
    piece_cols = mod_cols // n_dp
    mod_pieces = jnp.transpose(mod_part.reshape(latents, n_dp, piece_cols), (1, 0, 2))
    mod_piece = jnp.sum(
        lax.all_to_all(mod_pieces.reshape(n_dp, latents * piece_cols), DP, 0, 0), axis=0
    )
    modulation = spread(mod_piece, ALL, n_dp * group).reshape(n_dp, group, latents, piece_cols)
    modulation = jnp.transpose(modulation, (2, 1, 0, 3)).reshape(latents, 6 * width)
    one_hot = (segments[:, None] == jnp.arange(latents, dtype=jnp.int32)[None, :]).astype(F32)
    one_hot_s = own_rows(one_hot)

    def modulate(hot, first, last):
        return jnp.dot(
            hot, modulation[:, first * width : last * width], precision=lax.Precision.HIGHEST
        )

    shift_attn, scale_attn = jnp.split(modulate(one_hot, 0, 2), 2, axis=1)
    gate_mlp = modulate(one_hot, 5, 6)
    scale_attn_s, gate_attn_s, shift_mlp_s, scale_mlp_s, gate_mlp_s = jnp.split(
        modulate(one_hot_s, 1, 6), 5, axis=1
    )
    live = (jnp.arange(tok_rows, dtype=jnp.int32) < live_counts[0]).astype(F32)[:, None]
    live_s = own_rows(live)
    token_vals = tokens.astype(F32)
    token_s = own_rows(token_vals)
    normed_one, inv_one = normalize(token_vals)
    attn_input = (normed_one * (1.0 + scale_attn) + shift_attn).astype(BF)
    block_input = doubled(doubled(own_rows(attn_input), "db", 1), "db", 2)
    block_input = doubled(doubled(block_input, "mp", 2), "mp", 1)

    head_bias = attn_bias.reshape(2, heads_here, HD)
    bias_t = jnp.stack([jnp.zeros_like(head_bias[0]), head_bias[1], head_bias[0]], axis=1)
    kvq_t = (dot(attn_full, attn_input, 0, 1) + bias_t.reshape(3 * columns)[:, None]).astype(BF)
    kvq_t = kvq_t.reshape(heads_here, 3 * HD, tok_rows)
    tags = jnp.stack(
        [jnp.where(live[:, 0] > 0.0, segments + 1, 0).astype(BF), (segments + 1).astype(BF)]
    )
    tags = jnp.pad(tags, ((0, KV_ROWS - 2 * HD - 2), (0, 0)))
    tags = jnp.broadcast_to(tags[None], (heads_here,) + tags.shape)
    sent = jnp.concatenate([kvq_t[:, : 2 * HD], tags, kvq_t[:, 2 * HD :]], axis=1)
    got = lax.all_to_all(sent, "db", 0, 0)
    kv_own = got[:, :KV_ROWS]
    kv_all = jnp.stack([kv_own] + neighbours(kv_own, blocks))
    key_blocks = kv_all.shape[0]
    keys_seen = key_blocks * block_rows
    kv_t = jnp.transpose(kv_all, (2, 0, 1, 3)).reshape(KV_ROWS, keys_seen)
    key_t, value_t = kv_t[:HD], kv_t[HD : 2 * HD]
    key_tag = kv_t[2 * HD].astype(F32)
    query_tag = kv_t[2 * HD + 1, :block_rows].astype(F32)
    query_t = jnp.transpose(got[:, KV_ROWS:], (1, 0, 2)).reshape(HD, block_rows)
    self_mask = (
        jnp.arange(keys_seen, dtype=jnp.int32)[None, :]
        == jnp.arange(block_rows, dtype=jnp.int32)[:, None]
    )
    allowed = (key_tag[None, :] == query_tag[:, None]) | self_mask

    def masked_scores():
        return jnp.where(allowed, dot(query_t, key_t, 0, 0) * score_scale, NEG_FILL)

    scores = masked_scores()
    row_max = jnp.max(scores, axis=-1, keepdims=True)
    log_total = row_max + jnp.log(jnp.sum(jnp.exp(scores - row_max), axis=-1, keepdims=True))
    attn_exact = jnp.exp(scores - log_total)
    attn_probs = attn_exact.astype(BF)
    head_attended = dot(value_t, attn_probs, 1, 1).astype(BF)

    def to_owners(head_rows):
        rows = head_rows.shape[0]
        parts = jnp.transpose(head_rows.reshape(rows, BLOCK, tok_rows), (1, 0, 2))
        return lax.all_to_all(parts, "db", 0, 0).reshape(heads_here * rows, tok_rows)

    attended_t = to_owners(head_attended)
    attn_out_s = scatter_rows(dot(attended_t, out_t, 0, 1)) + out_bias
    mid_s = token_s + live_s * gate_attn_s * attn_out_s
    normed_two_s, inv_two_s = normalize(mid_s)
    mlp_input_s = (normed_two_s * (1.0 + scale_mlp_s) + shift_mlp_s).astype(BF)
    mlp_input = lax.all_gather(mlp_input_s, "mp", axis=0, tiled=True)
    hidden_pre = dot(mlp_input, up_full, 1, 0) + up_bias
    hidden = gelu_tanh(hidden_pre).astype(BF)

    grad_result = cotangent.astype(F32)
    grad_result_s = own_rows(grad_result)
    grad_mlp = grad_result * live * gate_mlp
    grad_mlp_b = grad_mlp.astype(BF)
    grad_hidden = dot(grad_mlp_b, down_t, 1, 0)
    grad_pre = jax.vjp(gelu_tanh, hidden_pre)[1](grad_hidden)[0]
    grad_pre_b = grad_pre.astype(BF)
    grad_mlp_in_s = scatter_rows(dot(grad_pre_b, up_full, 1, 1))
    grad_mid_s = grad_result_s + normalize_back(
        grad_mlp_in_s * (1.0 + scale_mlp_s), normed_two_s, inv_two_s
    )
    grad_attn_s = grad_mid_s * live_s * gate_attn_s
    grad_attn_b = lax.all_gather(grad_attn_s.astype(BF), "mp", axis=0, tiled=True)
    grad_down_w = dot(grad_mlp_b, hidden, 0, 0)
    grad_up_w = dot(mlp_input, grad_pre_b, 0, 0)
    mlp_w = lax.psum_scatter(
        jnp.concatenate([grad_up_w.astype(BF), grad_down_w.astype(BF)], axis=1),
        DP,
        scatter_dimension=0,
        tiled=True,
    )
    mlp_out_s = scatter_rows(dot(hidden, down_t, 1, 1)) + down_bias
    result_s = (mid_s + live_s * gate_mlp_s * mlp_out_s).astype(BF)

    grad_attended_t = dot(out_t, grad_attn_b, 0, 1).astype(BF)
    got_grad = lax.all_to_all(grad_attended_t.reshape(heads_here, HD, tok_rows), "db", 0, 0)
    grad_t = jnp.transpose(got_grad, (1, 0, 2)).reshape(HD, block_rows)
    grad_probs = dot(grad_t, value_t, 0, 0)
    delta = jnp.sum(grad_t.astype(F32) * head_attended.astype(F32), axis=0)[:, None]
    grad_scores = (attn_exact * (grad_probs - delta)).astype(BF)
    grad_query_t = dot(key_t, grad_scores, 1, 1) * score_scale
    grad_key_t = dot(query_t, grad_scores, 1, 0) * score_scale
    grad_value_t = dot(grad_t, attn_probs, 1, 0)
    grad_kv_t = jnp.concatenate([grad_key_t, grad_value_t])
    others = [
        grad_kv_t[:, i * block_rows : (i + 1) * block_rows].astype(BF)
        for i in range(1, key_blocks)
    ]
    grad_kv_own = grad_kv_t[:, :block_rows] + return_grads(others, blocks)
    attn_b_part = jnp.concatenate(
        [jnp.sum(grad_query_t, axis=1), jnp.sum(grad_kv_own[HD:], axis=1)]
    )
    head_grads = jnp.concatenate([grad_kv_own, grad_query_t]).astype(BF)
    grad_kvq_t = to_owners(head_grads)
    ordered = jnp.transpose(
        head_grads.reshape(3 * HD, BLOCK, 2, 2, share), (0, 3, 2, 1, 4)
    ).reshape(3 * HD, block_rows)
    grad_attn_w = dot(block_input, ordered, 0, 1)
    grad_out_w = dot(grad_attn_b, attended_t, 0, 1)
    terms = jnp.concatenate([grad_attn_w.astype(BF), grad_out_w.astype(BF)], axis=1)
    terms, mlp_w = lax.optimization_barrier((terms, mlp_w))
    up_w_out, down_w_out = mlp_w[:, :hidden_cols].astype(F32), mlp_w[:, hidden_cols:].T.astype(F32)
    terms = lax.all_to_all(terms.reshape(n_dp, weight_rows, 3 * HD + columns), DP, 0, 0)
    out_w_out = jnp.sum(terms[:, :, 3 * HD :].astype(F32), axis=0).T
    attn_w = terms[:, :, : 3 * HD].astype(F32).reshape(blocks, heads_here, weight_rows, 3, HD)
    attn_w = jnp.transpose(jnp.sum(attn_w, axis=0), (2, 1, 0, 3)).reshape(3, weight_rows, columns)
    attn_w_out = jnp.stack([attn_w[2], attn_w[0], attn_w[1]])
    grad_attn_in_s = scatter_rows(dot(grad_kvq_t, attn_full, 0, 1))
    normed_one_s = own_rows(normed_one)
    inv_one_s = own_rows(inv_one)
    grad_tokens_s = grad_mid_s + normalize_back(
        grad_attn_in_s * (1.0 + scale_attn_s), normed_one_s, inv_one_s
    )

    grad_mod_rows = jnp.concatenate(
        [
            grad_attn_in_s,
            grad_attn_in_s * normed_one_s,
            grad_mid_s * live_s * attn_out_s,
            grad_mlp_in_s,
            grad_mlp_in_s * normed_two_s,
            grad_result_s * live_s * mlp_out_s,
        ],
        axis=1,
    )
    grad_mod_share = jnp.dot(one_hot_s.T, grad_mod_rows, precision=lax.Precision.HIGHEST)
    pieces = jnp.transpose(
        grad_mod_share.reshape(latents, group, n_dp, piece_cols), (2, 1, 0, 3)
    ).reshape(n_dp * group, latents * piece_cols)
    up_piece = jnp.repeat(jnp.sum(grad_pre, axis=0).reshape(n_dp, -1), group, axis=0)
    both_part = jnp.concatenate([jnp.sum(own_rows(grad_mlp), axis=0), jnp.sum(grad_attn_s, axis=0)])
    both_piece = both_part.reshape(n_dp * group, -1)
    taken = lax.all_to_all(
        jnp.concatenate([pieces, both_piece, up_piece], axis=1), ALL, 0, 0
    )
    at = latents * piece_cols
    both_at = at + both_piece.shape[1]
    from_group = taken[:, both_at:].reshape(n_dp, group, -1)
    up_sum = jnp.sum(lax.dynamic_index_in_dim(from_group, member, 1, keepdims=False), axis=0)
    small = jnp.concatenate([jnp.sum(taken[:, :both_at], axis=0), up_sum, attn_b_part])
    small_all = spread(small, ALL, n_dp * group).reshape(n_dp, group, -1)
    small_own = lax.dynamic_index_in_dim(small_all, member, 1, keepdims=False)
    own_cols = jnp.transpose(
        small_own[:, :at].reshape(n_dp, latents, piece_cols), (1, 0, 2)
    ).reshape(latents, mod_cols)
    both_b = small_all[:, :, at:both_at].reshape(2 * width)
    down_b_all, out_b_all = both_b[:width], both_b[width:]
    up_at = both_at + up_sum.shape[0]
    up_b_out = small_own[:, both_at:up_at].reshape(hidden_cols)
    attn_b_own = small_own[:, up_at:].reshape(blocks, heads_here, 2, HD)
    attn_b_out = jnp.transpose(jnp.sum(attn_b_own, axis=0), (1, 0, 2)).reshape(2, columns)
    mod_w_out = jnp.dot(silu_own.astype(F32).T, own_cols, precision=lax.Precision.HIGHEST)
    mod_b_out = jnp.sum(own_cols, axis=0)
    silu_part = jnp.dot(own_cols, mod_weight.astype(F32).T, precision=lax.Precision.HIGHEST)
    silu_parts = spread(silu_part.reshape(-1), ALL, n_dp * group)
    silu_parts = jnp.sum(silu_parts.reshape(n_dp, group, latents, weight_rows), axis=1)
    grad_silu = jnp.transpose(silu_parts, (1, 0, 2)).reshape(latents, width)
    grad_conditioning = grad_silu * silu_slope(cond_vals)
    return (
        result_s,
        grad_tokens_s,
        grad_conditioning,
        attn_w_out,
        attn_b_out,
        out_w_out,
        out_b_all,
        up_w_out,
        up_b_out,
        down_w_out,
        down_b_all,
        mod_w_out,
        mod_b_out,
    )


def solution(mesh):
    n_dp = mesh.shape["dp"]
    fine = Mesh(mesh.devices.reshape(n_dp // BLOCK, BLOCK, mesh.shape["mp"]), ALL)
    placed = (
        P(DP, None),
        P(),
        P(DP),
        P(DP),
        P(None, DP, "mp"),
        P(None, "mp"),
        P("mp", DP),
        P(),
        P(DP, "mp"),
        P("mp"),
        P("mp", DP),
        P(),
        P(DP, "mp"),
        P("mp"),
        P(DP, None),
    )
    return jax.shard_map(
        shards,
        mesh=fine,
        in_specs=placed,
        out_specs=(
            P(ALL, None),
            P(ALL, None),
            P(),
            P(None, DP, "mp"),
            P(None, "mp"),
            P("mp", DP),
            P(),
            P(DP, "mp"),
            P("mp"),
            P("mp", DP),
            P(),
            P(DP, "mp"),
            P("mp"),
        ),
        check_vma=False,
    )
```
